32 devices in a mesh: dp: 4 (over y, x), expert: 8 (over z, core).
Axes of the slice: x: 2, y: 2, z: 4, core: 2. Of those that a mesh axis runs over, the one named last changes fastest.
Arguments:
- tokens: bfloat16 [256, 3584], P('expert', 'dp'), may hold values from -6 to 6
- upstream: bfloat16 [256, 3584], P('expert', 'dp'), may hold values from -6 to 6
- expert_ids: int32 [256, 8], P('expert'), may hold values from 0 to 31, all different within a row
- gates: float32 [256, 8], P('expert'), may hold values from 0.2 to 1
- hot: int32 [8], replicated, may hold values from 0 to 1, as said below
- w_in: bfloat16 [8, 3584, 2048], P('expert', 'dp'), may hold values from -0.09375 to 0.09375
- w_down: bfloat16 [8, 1024, 3584], P('expert', None, 'dp'), may hold values from -0.1875 to 0.1875
Outputs:
- layer_out: bfloat16 [256, 3584], P('expert', 'dp')
- token_grad: bfloat16 [256, 3584], P('expert', 'dp')
- grad_in: bfloat16 [8, 3584, 2048], P('expert', 'dp')
- grad_down: bfloat16 [8, 1024, 3584], P('expert', None, 'dp')
The draws below stay inside these ranges and needn't reach their ends.
Inputs may be any that keep to these rules, and one draw needn't show every extreme that they name: `expert_ids`: each row names 8 different experts; only those below 8 are computed by this layer. Every expert below 4 is hot; the others may or may not be.
All inputs are finite; a program needn't handle non-finite values.
Results may differ from the reference program's by a relative error of at most 0.028.
Values may be sent and summed in bfloat16 or wider, within the bound.
No kernel may reach another device: no remote copies, remote signals or barrier semaphores. Data moves between devices by JAX's collectives and lax.ppermute only.
A program may use at most 64 MiB of HBM per device.

```python
import jax
import jax.numpy as jnp
from jax import lax

D = 3584
H = 1024
TOP = 8
CAP = 2
EXPERTS = 8
E_ALL = 32
TOK_DEV = 32
TOKENS = 256
N_DP = 4
N_EXPERT = 8


def draw_hot(key, part):
    upper = jax.random.randint(jax.random.fold_in(key, 7), (EXPERTS,), 0, 2).astype(jnp.int32)
    lane = jnp.arange(EXPERTS, dtype=jnp.int32)
    return jnp.where(lane < EXPERTS // 2, 1, upper).astype(jnp.int32)


def level_of(own_key, extent, split, low, top_value):
    level, own = 1.0, jax.random.fold_in(own_key, 6)
    for dim, parts in split:
        draws = jnp.exp(jax.random.uniform(jax.random.fold_in(own, dim), (parts,), jnp.float32, low / len(split), top_value / len(split)))
        level = level * jnp.repeat(draws, extent[dim] // parts).reshape([-1 if axis == dim else 1 for axis in range(len(extent))])
    return level


def distinct(key, rows, number_of, top, lift):
    order = jax.random.permutation(jax.random.fold_in(key, 1), number_of)
    boost = order
    for power in range(3):
        boost = boost * boost // number_of
    boost = boost * lift // number_of
    tickets = jax.random.randint(jax.random.fold_in(key, 2), (rows, number_of), 0, 4096) + boost
    sure = jax.random.permutation(jax.random.fold_in(key, 3), rows)[jnp.arange(number_of) % rows]
    tickets = jnp.where(jnp.arange(rows)[:, None] == sure[None, :], 1 << 14, tickets)
    score = tickets * number_of + jnp.arange(number_of)
    return lax.top_k(score.astype(jnp.int32), top)[1].astype(jnp.int32)


def gaussian(stream_key, shape, deviation, limit, cuts=(), held_as=jnp.bfloat16):
    gain = level_of(stream_key, shape, cuts, -0.22, 0.18) if cuts else 1.0
    values = jax.random.normal(stream_key, shape, jnp.float32) * deviation * gain
    return jnp.minimum(jnp.maximum(values, -limit), limit).astype(held_as)


def setup_inputs(seed: int = 0) -> dict:
    arg_keys = jax.random.split(jax.random.key(seed), 8)
    return {
        "tokens": gaussian(arg_keys[0], (TOKENS, D), 1.0, 6.0, ((0, 8), (1, 4))),
        "upstream": gaussian(arg_keys[1], (TOKENS, D), 1.0, 6.0, ((0, 8), (1, 4))),
        "expert_ids": distinct(arg_keys[2], TOKENS, E_ALL, TOP, 4096),
        "gates": jnp.clip(0.2 + 0.8 * jax.random.uniform(arg_keys[3], (TOKENS, TOP), jnp.float32) ** level_of(arg_keys[3], (TOKENS, TOP), ((0, 8),), -0.2, 0.2), 0.2, 1.0),
        "hot": draw_hot(jax.random.fold_in(arg_keys[7], 71), 0),
        "w_in": gaussian(arg_keys[5], (EXPERTS, D, 2 * H), D ** -0.5, 0.09375, ((0, 8), (1, 4))),
        "w_down": gaussian(arg_keys[6], (EXPERTS, H, D), H ** -0.5, 0.1875, ((0, 8), (2, 4))),
    }


def plan_block(flat_ids, hot, expert_count, capacity):
    expert_lane = jnp.arange(expert_count, dtype=jnp.int32)
    in_window = flat_ids < expert_count
    chosen = ((flat_ids[:, None] == expert_lane[None, :]) & in_window[:, None]).astype(jnp.int32)
    occurrence = jnp.sum((jnp.cumsum(chosen, axis=0) - chosen) * chosen, axis=1)
    marked = jnp.sum(chosen * hot[None, :], axis=1)
    replica = (marked > 0) & (occurrence % 2 == 1)
    expert = jnp.where(in_window, flat_ids, 0)
    host_column = jnp.where(replica, (expert + expert_count // 2) % expert_count, expert)
    region_key = host_column + replica.astype(jnp.int32) * expert_count
    key_lane = jnp.arange(2 * expert_count, dtype=jnp.int32)
    keyed = ((region_key[:, None] == key_lane[None, :]) & in_window[:, None]).astype(jnp.int32)
    slot_rank = jnp.sum((jnp.cumsum(keyed, axis=0) - keyed) * keyed, axis=1)
    retained = in_window & (slot_rank < capacity)
    return expert, host_column, slot_rank, replica, retained


def round_trip(values):
    return lax.optimization_barrier(values.astype(jnp.bfloat16)).astype(jnp.float32)


def contract_first(left, right):
    return lax.dot_general(left, right, (((0,), (0,)), ((), ())), preferred_element_type=jnp.float32)


def reference(tokens, upstream, expert_ids, gates, hot, w_in, w_down):
    expert_count = EXPERTS
    sources = N_EXPERT
    block_size = TOK_DEV * TOP
    group_slots = 2 * sources * CAP
    half_slots = sources * CAP
    feature_block = D // N_DP
    flat_ids = expert_ids.reshape(sources, block_size)
    expert, host_column, slot_rank, replica, retained = jax.vmap(
        lambda ids_block: plan_block(ids_block, hot, expert_count, CAP))(flat_ids)
    source = jnp.arange(sources, dtype=jnp.int32)[:, None]
    slot = replica.astype(jnp.int32) * half_slots + source * CAP + slot_rank
    total_slots = expert_count * group_slots
    counts = TOKENS * TOP
    position = jnp.where(retained, expert * group_slots + slot, total_slots).reshape(-1).astype(jnp.int32)
    slot_index = jnp.full((total_slots + 1,), counts, jnp.int32)
    slot_index = slot_index.at[position].set(jnp.arange(counts, dtype=jnp.int32))
    slot_index = slot_index[:total_slots].reshape(expert_count, group_slots)
    flat_gates = gates.reshape(-1)

    def one_expert(inputs):
        index_row, weight_in, weight_down = inputs
        usable = index_row < counts
        safe_index = jnp.where(usable, index_row, 0)
        token_row = safe_index // TOP
        rows_in = jnp.where(usable[:, None], tokens[token_row], jnp.zeros((), tokens.dtype))
        scaled = flat_gates[safe_index][:, None] * upstream[token_row].astype(jnp.float32)
        rows_grad = jnp.where(usable[:, None], scaled, 0.0).astype(jnp.bfloat16)
        proj_pieces = jnp.einsum("rgk,gkc->rgc",
                                 rows_in.reshape(group_slots, N_DP, feature_block).astype(jnp.float32),
                                 weight_in.reshape(N_DP, feature_block, 2 * H).astype(jnp.float32))
        projected = jnp.sum(round_trip(proj_pieces), axis=1)
        gate_part = projected[:, :H]
        up_part = projected[:, H:]
        sigmoid_gate = jax.nn.sigmoid(gate_part)
        hidden = (gate_part * sigmoid_gate * up_part).astype(jnp.bfloat16)
        expert_out = jnp.dot(hidden, weight_down, preferred_element_type=jnp.float32).astype(jnp.bfloat16)
        grad_pieces = jnp.einsum("rgk,hgk->rgh",
                                 rows_grad.reshape(group_slots, N_DP, feature_block).astype(jnp.float32),
                                 weight_down.reshape(H, N_DP, feature_block).astype(jnp.float32))
        hidden_grad = jnp.sum(round_trip(grad_pieces), axis=1)
        gate_grad = hidden_grad * up_part * sigmoid_gate * (1.0 + gate_part * (1.0 - sigmoid_gate))
        up_grad = hidden_grad * gate_part * sigmoid_gate
        pair_grad = jnp.concatenate([gate_grad, up_grad], axis=1).astype(jnp.bfloat16)
        expert_input = lax.dot_general(pair_grad, weight_in, (((1,), (1,)), ((), ())),
                                       preferred_element_type=jnp.float32).astype(jnp.bfloat16)
        in_primary = contract_first(rows_in[:half_slots], pair_grad[:half_slots])
        in_replica = round_trip(contract_first(rows_in[half_slots:], pair_grad[half_slots:]))
        grad_in_one = (in_primary + in_replica).astype(jnp.bfloat16)
        down_primary = contract_first(hidden[:half_slots], rows_grad[:half_slots])
        down_replica = round_trip(contract_first(hidden[half_slots:], rows_grad[half_slots:]))
        grad_down_one = (down_primary + down_replica).astype(jnp.bfloat16)
        return expert_out, expert_input, grad_in_one, grad_down_one

    expert_out, expert_input, grad_in, grad_down = lax.map(one_expert, (slot_index, w_in, w_down))
    flat_out = expert_out.reshape(total_slots, -1)
    flat_input = expert_input.reshape(total_slots, -1)
    lookup = jnp.where(position < total_slots, position, 0)
    keep = retained.reshape(-1)[:, None]
    picked_out = jnp.where(keep, flat_out[lookup].astype(jnp.float32), 0.0)
    picked_input = jnp.where(keep, flat_input[lookup].astype(jnp.float32), 0.0)
    layer_out = jnp.sum((picked_out * flat_gates[:, None]).reshape(TOKENS, TOP, -1), axis=1).astype(jnp.bfloat16)
    token_grad = jnp.sum(picked_input.reshape(TOKENS, TOP, -1), axis=1).astype(jnp.bfloat16)
    return layer_out, token_grad, grad_in, grad_down
```

```python
import functools

import jax
import jax.numpy as jnp
from jax import lax
from jax.experimental import pallas as pl
from jax.experimental.pallas import tpu as pltpu
from jax.sharding import PartitionSpec as P

CAP = 2
SLOTS = 2 * CAP
PACK = 2 * SLOTS


def select_table(ids, gates, hot, rows):
    top, tokens = ids.shape
    experts = rows // PACK
    expert = lax.broadcasted_iota(jnp.int32, (rows, tokens), 0) // PACK
    wanted = lax.broadcasted_iota(jnp.int32, (rows, tokens), 0) % SLOTS
    chosen = jnp.zeros((rows, tokens), jnp.float32)
    gate = jnp.zeros((rows, tokens), jnp.float32)
    for k in range(top):
        hit = ids[k : k + 1, :] == expert
        chosen = jnp.where(hit, 1.0, chosen)
        gate = jnp.where(hit, gates[k : k + 1, :], gate)
    before = (
        lax.broadcasted_iota(jnp.int32, (tokens, tokens), 0)
        < lax.broadcasted_iota(jnp.int32, (tokens, tokens), 1)
    ).astype(jnp.float32).astype(jnp.bfloat16)
    occurrence = jnp.dot(
        chosen.astype(jnp.bfloat16), before, preferred_element_type=jnp.float32
    ).astype(jnp.int32)
    lane = lax.broadcasted_iota(jnp.int32, (rows, experts), 1)
    owner = lax.broadcasted_iota(jnp.int32, (rows, experts), 0) // PACK
    is_hot = jnp.max(jnp.where(lane == owner, hot, 0), axis=1, keepdims=True) == 1
    replica = jnp.where(is_hot, occurrence % 2, 0)
    rank = jnp.where(is_hot, occurrence // 2, occurrence)
    fills = (chosen > 0.0) & (rank < CAP) & (replica * CAP + rank == wanted)
    pick = jnp.where(fills, 1.0, 0.0)
    return pick, jnp.where(fills, gate, 0.0)


def dispatch_kernel(ids_ref, gates_ref, hot_ref, tokens_ref, upstream_ref, packed_ref):
    rows = packed_ref.shape[0]
    pick, gate = select_table(ids_ref[...], gates_ref[...], hot_ref[...], rows)
    part = (lax.broadcasted_iota(jnp.int32, (rows, 1), 0) % PACK) >= SLOTS
    pick = pick.astype(jnp.bfloat16)
    row_in = jnp.dot(pick, tokens_ref[...], preferred_element_type=jnp.float32)
    row_up = jnp.dot(pick, upstream_ref[...], preferred_element_type=jnp.float32)
    scale = jnp.sum(gate, axis=1, keepdims=True)
    packed_ref[...] = jnp.where(part, row_up * scale, row_in).astype(jnp.bfloat16)


def combine_kernel(ids_ref, gates_ref, hot_ref, back_ref, out_ref, grad_ref):
    rows = back_ref.shape[0]
    pick, gate = select_table(ids_ref[...], gates_ref[...], hot_ref[...], rows)
    part = (lax.broadcasted_iota(jnp.int32, (rows, 1), 0) % PACK) >= SLOTS
    gate = jnp.where(part, 0.0, gate)
    pick = jnp.where(part, pick, 0.0).astype(jnp.bfloat16)
    back = back_ref[...]
    dims = (((0,), (0,)), ((), ()))
    high = gate.astype(jnp.bfloat16)
    rest = gate - high.astype(jnp.float32)
    middle = rest.astype(jnp.bfloat16)
    low = (rest - middle.astype(jnp.float32)).astype(jnp.bfloat16)
    total = lax.dot_general(low, back, dims, preferred_element_type=jnp.float32)
    total += lax.dot_general(middle, back, dims, preferred_element_type=jnp.float32)
    total += lax.dot_general(high, back, dims, preferred_element_type=jnp.float32)
    out_ref[...] = total.astype(jnp.bfloat16)
    grad_ref[...] = lax.dot_general(
        pick, back, dims, preferred_element_type=jnp.float32
    ).astype(jnp.bfloat16)


def contract_last(left, right):
    return lax.dot_general(
        left, right, (((1,), (1,)), ((), ())), preferred_element_type=jnp.float32
    )


def contract_first(left, right):
    return lax.dot_general(
        left, right, (((0,), (0,)), ((), ())), preferred_element_type=jnp.float32
    )


def sum_over(pieces, axis, members):
    if members > 4 or members & (members - 1):
        return lax.psum(pieces, axis).astype(jnp.float32)
    total = pieces.astype(jnp.float32)
    for step in reversed(range(1, members)):
        pairs = [(i, i ^ step) for i in range(members)]
        total = total + lax.ppermute(pieces, axis, pairs).astype(jnp.float32)
    return total


def body(members, tokens, upstream, expert_ids, gates, hot, w_in, w_down):
    expert_count = hot.shape[0]
    token_count, top_count = expert_ids.shape
    share = tokens.shape[1]
    half = w_down.shape[1]
    rows = expert_count * PACK
    row_count = expert_count * SLOTS
    ids_t, gates_t, hot_row = expert_ids.T, gates.T, hot[None, :]
    own_in, own_down = w_in[0], w_down[0]
    packed = pl.pallas_call(
        dispatch_kernel,
        out_shape=jax.ShapeDtypeStruct((rows, share), jnp.bfloat16),
    )(ids_t, gates_t, hot_row, tokens, upstream)
    sent = lax.all_to_all(
        packed.reshape(expert_count, PACK, share),
        "expert", split_axis=0, concat_axis=0, tiled=True,
    )
    rows_in = sent[:, :SLOTS].reshape(row_count, share)
    rows_grad = sent[:, SLOTS:].reshape(row_count, share)
    pieces = jnp.concatenate(
        [
            jnp.dot(rows_in, own_in, preferred_element_type=jnp.float32).astype(jnp.bfloat16),
            contract_last(rows_grad, own_down).astype(jnp.bfloat16),
        ],
        axis=1,
    )
    total = sum_over(pieces, "dp", members)
    gate_part = total[:, :half]
    up_part = total[:, half : 2 * half]
    hidden_grad = total[:, 2 * half :]
    sigmoid_gate = jax.nn.sigmoid(gate_part)
    hidden = (gate_part * sigmoid_gate * up_part).astype(jnp.bfloat16)
    gate_grad = hidden_grad * up_part * sigmoid_gate * (1.0 + gate_part * (1.0 - sigmoid_gate))
    up_grad = hidden_grad * gate_part * sigmoid_gate
    pair_grad = jnp.concatenate([gate_grad, up_grad], axis=1).astype(jnp.bfloat16)
    out_rows = jnp.dot(hidden, own_down, preferred_element_type=jnp.float32).astype(jnp.bfloat16)
    input_rows = contract_last(pair_grad, own_in).astype(jnp.bfloat16)
    grad_in = contract_first(rows_in, pair_grad).astype(jnp.bfloat16)
    grad_down = contract_first(hidden, rows_grad).astype(jnp.bfloat16)
    back = lax.all_to_all(
        jnp.concatenate(
            [
                out_rows.reshape(expert_count, SLOTS, share),
                input_rows.reshape(expert_count, SLOTS, share),
            ],
            axis=1,
        ),
        "expert", split_axis=0, concat_axis=0, tiled=True,
    )
    layer_out, token_grad = pl.pallas_call(
        combine_kernel,
        out_shape=[jax.ShapeDtypeStruct((token_count, share), jnp.bfloat16)] * 2,
    )(ids_t, gates_t, hot_row, back.reshape(rows, share))
    return (layer_out, token_grad, grad_in[None], grad_down[None])


def solution(mesh):
    return jax.shard_map(
        functools.partial(body, mesh.shape["dp"]),
        mesh=mesh,
        in_specs=(
            P("expert", "dp"),
            P("expert", "dp"),
            P("expert", None),
            P("expert", None),
            P(),
            P("expert", "dp", None),
            P("expert", None, "dp"),
        ),
        out_specs=(
            P("expert", "dp"),
            P("expert", "dp"),
            P("expert", "dp", None),
            P("expert", None, "dp"),
        ),
        check_vma=False,
    )
```

```python
import functools

import jax
import jax.numpy as jnp
from jax import lax
from jax.experimental import pallas as pl
from jax.experimental.pallas import tpu as pltpu
from jax.sharding import PartitionSpec as P

CAP = 2
SLOTS = 2 * CAP
PACK = 2 * SLOTS
VMEM_LIMIT = 24 << 20


def select_table(ids, gates, hot, rows):
    top, tokens = ids.shape
    experts = rows // PACK
    expert = lax.broadcasted_iota(jnp.int32, (rows, tokens), 0) // PACK
    wanted = lax.broadcasted_iota(jnp.int32, (rows, tokens), 0) % SLOTS
    chosen = jnp.zeros((rows, tokens), jnp.float32)
    gate = jnp.zeros((rows, tokens), jnp.float32)
    for k in range(top):
        hit = ids[k : k + 1, :] == expert
        chosen = jnp.where(hit, 1.0, chosen)
        gate = jnp.where(hit, gates[k : k + 1, :], gate)
    before = (
        lax.broadcasted_iota(jnp.int32, (tokens, tokens), 0)
        < lax.broadcasted_iota(jnp.int32, (tokens, tokens), 1)
    ).astype(jnp.float32).astype(jnp.bfloat16)
    occurrence = jnp.dot(
        chosen.astype(jnp.bfloat16), before, preferred_element_type=jnp.float32
    ).astype(jnp.int32)
    lane = lax.broadcasted_iota(jnp.int32, (rows, experts), 1)
    owner = lax.broadcasted_iota(jnp.int32, (rows, experts), 0) // PACK
    is_hot = jnp.max(jnp.where(lane == owner, hot, 0), axis=1, keepdims=True) == 1
    replica = jnp.where(is_hot, occurrence % 2, 0)
    rank = jnp.where(is_hot, occurrence // 2, occurrence)
    fills = (chosen > 0.0) & (rank < CAP) & (replica * CAP + rank == wanted)
    pick = jnp.where(fills, 1.0, 0.0)
    return pick, jnp.where(fills, gate, 0.0)


def part_of(rows):
    return (lax.broadcasted_iota(jnp.int32, (rows, 1), 0) % PACK) // SLOTS


def part_of(rows):
    return (lax.broadcasted_iota(jnp.int32, (rows, 1), 0) % PACK) // SLOTS


def dispatch_kernel(
    ids_hbm, gates_hbm, hot_hbm, tokens_hbm, upstream_hbm, w_in_hbm,
    packed_ref, pick_ref, gate_ref, w_in_ref,
    ids_ref, gates_ref, hot_ref, tokens_ref, upstream_ref, sems,
):
    sources = (ids_hbm, gates_hbm, hot_hbm, tokens_hbm, upstream_hbm, w_in_hbm)
    targets = (ids_ref, gates_ref, hot_ref, tokens_ref, upstream_ref, w_in_ref)
    copies = [
        pltpu.make_async_copy(source, target, sems.at[i])
        for i, (source, target) in enumerate(zip(sources, targets))
    ]
    for copy in copies:
        copy.start()
    for copy in copies[:3]:
        copy.wait()
    rows = packed_ref.shape[0]
    pick, gate = select_table(ids_ref[...], gates_ref[...], hot_ref[...], rows)
    is_grad = part_of(rows) == 1
    pick = pick.astype(jnp.bfloat16)
    scale = jnp.sum(gate, axis=1, keepdims=True)
    pick_ref[...] = pick
    gate_ref[...] = gate
    for copy in copies[3:5]:
        copy.wait()
    row_in = jnp.dot(pick, tokens_ref[...], preferred_element_type=jnp.float32)
    row_up = jnp.dot(pick, upstream_ref[...], preferred_element_type=jnp.float32)
    packed_ref[...] = jnp.where(is_grad, row_up * scale, row_in).astype(jnp.bfloat16)
    copies[5].wait()


def spread(rows, part):
    row = lax.broadcasted_iota(jnp.int32, (rows, rows // 2), 0)
    column = lax.broadcasted_iota(jnp.int32, (rows, rows // 2), 1)
    place = (column // SLOTS) * PACK + part * SLOTS + column % SLOTS
    return jnp.where(row == place, 1.0, 0.0).astype(jnp.bfloat16)


def gather(rows, part):
    row = lax.broadcasted_iota(jnp.int32, (rows // 2, rows), 1)
    column = lax.broadcasted_iota(jnp.int32, (rows // 2, rows), 0)
    place = (column // SLOTS) * PACK + part * SLOTS + column % SLOTS
    return jnp.where(row == place, 1.0, 0.0).astype(jnp.bfloat16)


def forward_kernel(sent_ref, w_in_ref, w_down_ref, pieces_ref, rows_in_ref, rows_grad_ref):
    rows, wide = sent_ref.shape[0], w_in_ref.shape[1]
    sent = sent_ref[...]
    rows_in = jnp.dot(
        gather(rows, 0), sent, preferred_element_type=jnp.float32
    ).astype(jnp.bfloat16)
    rows_grad = jnp.dot(
        gather(rows, 1), sent, preferred_element_type=jnp.float32
    ).astype(jnp.bfloat16)
    rows_in_ref[...] = rows_in
    rows_grad_ref[...] = rows_grad
    pieces_ref[:, wide:] = contract_last(rows_grad, w_down_ref[...]).astype(jnp.bfloat16)
    pieces_ref[:, :wide] = jnp.dot(
        rows_in, w_in_ref[...], preferred_element_type=jnp.float32
    ).astype(jnp.bfloat16)


def backward_kernel(count, *refs):
    piece_refs = refs[:count]
    w_in_ref, w_down_ref, hidden_ref, pair_ref, back_ref = refs[count:]
    rows, half = back_ref.shape[0], hidden_ref.shape[1]
    total = piece_refs[0][...].astype(jnp.float32)
    for piece_ref in piece_refs[1:]:
        total = total + piece_ref[...].astype(jnp.float32)
    gate_part = total[:, :half]
    up_part = total[:, half : 2 * half]
    hidden_grad = total[:, 2 * half :]
    sigmoid_gate = jax.nn.sigmoid(gate_part)
    swish = gate_part * sigmoid_gate
    hidden = (swish * up_part).astype(jnp.bfloat16)
    gate_grad = hidden_grad * up_part * sigmoid_gate * (1.0 + gate_part * (1.0 - sigmoid_gate))
    hidden_ref[...] = hidden
    pair_ref[:, :half] = gate_grad.astype(jnp.bfloat16)
    pair_ref[:, half:] = (hidden_grad * swish).astype(jnp.bfloat16)
    out_rows = jnp.dot(
        hidden, w_down_ref[...], preferred_element_type=jnp.float32
    ).astype(jnp.bfloat16)
    input_rows = contract_last(pair_ref[...], w_in_ref[...]).astype(jnp.bfloat16)
    back_ref[...] = (
        jnp.dot(spread(rows, 0), out_rows, preferred_element_type=jnp.float32)
        + jnp.dot(spread(rows, 1), input_rows, preferred_element_type=jnp.float32)
    ).astype(jnp.bfloat16)


def combine_kernel(pick_ref, gate_ref, back_ref, out_ref, grad_ref):
    rows = back_ref.shape[0]
    is_grad = part_of(rows) == 1
    gate = jnp.where(is_grad, 0.0, gate_ref[...])
    pick = jnp.where(is_grad, pick_ref[...].astype(jnp.float32), 0.0).astype(jnp.bfloat16)
    back = back_ref[...]
    high = gate.astype(jnp.bfloat16)
    rest = gate - high.astype(jnp.float32)
    middle = rest.astype(jnp.bfloat16)
    low = (rest - middle.astype(jnp.float32)).astype(jnp.bfloat16)
    total = contract_first(low, back) + contract_first(middle, back) + contract_first(high, back)
    out_ref[...] = total.astype(jnp.bfloat16)
    grad_ref[...] = contract_first(pick, back).astype(jnp.bfloat16)


def on_chip(array):
    return pltpu.with_memory_space_constraint(array, pltpu.VMEM)


def off_chip(array):
    return pltpu.with_memory_space_constraint(array, pltpu.HBM)


def contract_last(left, right):
    return lax.dot_general(
        left, right, (((1,), (1,)), ((), ())), preferred_element_type=jnp.float32
    )


def contract_first(left, right):
    return lax.dot_general(
        left, right, (((0,), (0,)), ((), ())), preferred_element_type=jnp.float32
    )


def pieces_over(pieces, axis, members):
    if members > 4 or members & (members - 1):
        return [lax.psum(pieces, axis)]
    found = [pieces]
    for step in reversed(range(1, members)):
        found.append(lax.ppermute(pieces, axis, [(i, i ^ step) for i in range(members)]))
    return found


def body(members, tokens, upstream, expert_ids, gates, hot, w_in, w_down):
    expert_count = hot.shape[0]
    token_count, top_count = expert_ids.shape
    share = tokens.shape[1]
    half, wide = w_down.shape[1], w_in.shape[2]
    rows = expert_count * PACK
    row_count = expert_count * SLOTS
    own_in, own_down = w_in[0], w_down[0]
    params = pltpu.CompilerParams(vmem_limit_bytes=VMEM_LIMIT)
    small = (expert_ids.T, gates.T, hot[None, :], tokens, upstream)
    packed, pick, gate, near_in = pl.pallas_call(
        dispatch_kernel,
        in_specs=[pl.BlockSpec(memory_space=pl.ANY)] * 6,
        out_shape=[
            pltpu.VMEM((rows, share), jnp.bfloat16),
            pltpu.VMEM((rows, token_count), jnp.bfloat16),
            pltpu.VMEM((rows, token_count), jnp.float32),
            pltpu.VMEM(own_in.shape, jnp.bfloat16),
        ],
        scratch_shapes=[pltpu.VMEM(x.shape, x.dtype) for x in small]
        + [pltpu.SemaphoreType.DMA((6,))],
        compiler_params=params,
    )(*[off_chip(x) for x in small + (own_in,)])
    sent = lax.all_to_all(
        packed.reshape(expert_count, PACK, share),
        "expert", split_axis=0, concat_axis=0, tiled=True,
    ).reshape(rows, share)
    pieces, rows_in, rows_grad = pl.pallas_call(
        forward_kernel,
        out_shape=[
            pltpu.VMEM((row_count, wide + half), jnp.bfloat16),
            pltpu.VMEM((row_count, share), jnp.bfloat16),
            pltpu.VMEM((row_count, share), jnp.bfloat16),
        ],
        compiler_params=params,
    )(on_chip(sent), on_chip(near_in), own_down)
    found = pieces_over(pieces, "dp", members)
    hidden, pair_grad, answer = pl.pallas_call(
        functools.partial(backward_kernel, len(found)),
        out_shape=[
            pltpu.VMEM((row_count, half), jnp.bfloat16),
            pltpu.VMEM((row_count, wide), jnp.bfloat16),
            pltpu.VMEM((rows, share), jnp.bfloat16),
        ],
        compiler_params=params,
    )(*[on_chip(piece) for piece in found], on_chip(near_in), own_down)
    back = lax.all_to_all(
        answer.reshape(expert_count, PACK, share),
        "expert", split_axis=0, concat_axis=0, tiled=True,
    ).reshape(rows, share)
    grad_in = contract_first(rows_in, pair_grad).astype(jnp.bfloat16)
    grad_down = contract_first(hidden, rows_grad).astype(jnp.bfloat16)
    layer_out, token_grad = pl.pallas_call(
        combine_kernel,
        out_shape=[jax.ShapeDtypeStruct((token_count, share), jnp.bfloat16)] * 2,
        compiler_params=params,
    )(on_chip(pick), on_chip(gate), on_chip(back))
    return (layer_out, token_grad, grad_in[None], grad_down[None])


def solution(mesh):
    return jax.shard_map(
        functools.partial(body, mesh.shape["dp"]),
        mesh=mesh,
        in_specs=(
            P("expert", "dp"),
            P("expert", "dp"),
            P("expert", None),
            P("expert", None),
            P(),
            P("expert", "dp", None),
            P("expert", None, "dp"),
        ),
        out_specs=(
            P("expert", "dp"),
            P("expert", "dp"),
            P("expert", "dp", None),
            P("expert", None, "dp"),
        ),
        check_vma=False,
    )
```

```python
import functools

import jax
import jax.numpy as jnp
from jax import lax
from jax.experimental import pallas as pl
from jax.experimental.pallas import tpu as pltpu
from jax.sharding import PartitionSpec as P

CAP = 2
SLOTS = 2 * CAP
PACK = 2 * SLOTS
VMEM_LIMIT = 24 << 20


def select_table(ids, gates, hot, owner):
    top, tokens = ids.shape
    rows, experts = owner.shape[0], hot.shape[1]
    wanted = lax.broadcasted_iota(jnp.int32, (rows, 1), 0) % SLOTS
    chosen = jnp.zeros((rows, tokens), jnp.float32)
    gate = jnp.zeros((rows, tokens), jnp.float32)
    for k in range(top):
        hit = ids[k : k + 1, :] == owner
        chosen = jnp.where(hit, 1.0, chosen)
        gate = jnp.where(hit, gates[k : k + 1, :], gate)
    before = (
        lax.broadcasted_iota(jnp.int32, (tokens, tokens), 0)
        < lax.broadcasted_iota(jnp.int32, (tokens, tokens), 1)
    ).astype(jnp.float32).astype(jnp.bfloat16)
    occurrence = jnp.dot(
        chosen.astype(jnp.bfloat16), before, preferred_element_type=jnp.float32
    ).astype(jnp.int32)
    lane = lax.broadcasted_iota(jnp.int32, (rows, experts), 1)
    is_hot = jnp.max(jnp.where(lane == owner, hot, 0), axis=1, keepdims=True) == 1
    replica = jnp.where(is_hot, occurrence % 2, 0)
    rank = jnp.where(is_hot, occurrence // 2, occurrence)
    fills = (chosen > 0.0) & (rank < CAP) & (replica * CAP + rank == wanted)
    pick = jnp.where(fills, 1.0, 0.0)
    return pick, jnp.where(fills, gate, 0.0)


def part_of(rows):
    return (lax.broadcasted_iota(jnp.int32, (rows, 1), 0) % PACK) // SLOTS


def part_of(rows):
    return (lax.broadcasted_iota(jnp.int32, (rows, 1), 0) % PACK) // SLOTS


def owner_of(rows, fold, paired):
    group = lax.broadcasted_iota(jnp.int32, (rows, 1), 0) // PACK
    if not fold:
        return group
    if not paired:
        half = rows // PACK // 2
        group = 2 * (group % half) + group // half
    return lax.axis_index("expert") ^ group


def dispatch_kernel(
    fold, ids_hbm, gates_hbm, hot_hbm, tokens_hbm, upstream_hbm,
    packed_ref, pick_ref, gate_ref,
    ids_ref, gates_ref, hot_ref, tokens_ref, upstream_ref, sems,
):
    sources = (ids_hbm, gates_hbm, hot_hbm, tokens_hbm, upstream_hbm)
    targets = (ids_ref, gates_ref, hot_ref, tokens_ref, upstream_ref)
    copies = [
        pltpu.make_async_copy(source, target, sems.at[i])
        for i, (source, target) in enumerate(zip(sources, targets))
    ]
    for copy in copies:
        copy.start()
    for copy in copies[:3]:
        copy.wait()
    rows = packed_ref.shape[0]
    pick, gate = select_table(
        ids_ref[...], gates_ref[...], hot_ref[...], owner_of(rows, fold, False)
    )
    is_grad = part_of(rows) == 1
    pick_ref[...] = pick
    gate_ref[...] = gate
    pick = pick.astype(jnp.bfloat16)
    scale = jnp.sum(gate, axis=1, keepdims=True)
    for copy in copies[3:]:
        copy.wait()
    row_in = jnp.dot(pick, tokens_ref[...], preferred_element_type=jnp.float32)
    row_up = jnp.dot(pick, upstream_ref[...], preferred_element_type=jnp.float32)
    packed_ref[...] = jnp.where(is_grad, row_up * scale, row_in).astype(jnp.bfloat16)


def gather(rows, part):
    row = lax.broadcasted_iota(jnp.int32, (rows // 2, rows), 1)
    column = lax.broadcasted_iota(jnp.int32, (rows // 2, rows), 0)
    place = (column // SLOTS) * PACK + part * SLOTS + column % SLOTS
    return jnp.where(row == place, 1.0, 0.0).astype(jnp.bfloat16)


def spread(rows, part, fold):
    row = lax.broadcasted_iota(jnp.int32, (rows, rows // 2), 0)
    column = lax.broadcasted_iota(jnp.int32, (rows, rows // 2), 1)
    group = column // SLOTS
    if fold:
        group = (group % 2) * (rows // PACK // 2) + group // 2
    place = group * PACK + part * SLOTS + column % SLOTS
    return jnp.where(row == place, 1.0, 0.0).astype(jnp.bfloat16)


def load_kernel(after_ref, w_in_hbm, w_down_hbm, w_in_ref, w_down_ref, sems):
    loads = [
        pltpu.make_async_copy(w_in_hbm, w_in_ref, sems.at[0]),
        pltpu.make_async_copy(w_down_hbm, w_down_ref, sems.at[1]),
    ]
    for load in loads:
        load.start()
    for load in loads:
        load.wait()


def together(refs):
    if len(refs) == 1:
        return refs[0][...]
    parts = [refs[0][:PACK], refs[1][:PACK]] + [ref[...] for ref in refs[2:]]
    return jnp.concatenate(parts, axis=0)


def forward_kernel(*refs):
    w_in_ref, w_down_ref, proj_ref, grad_ref, rows_in_ref, rows_grad_ref = refs[-6:]
    sent = together(refs[:-6])
    rows = sent.shape[0]
    rows_in = jnp.dot(
        gather(rows, 0), sent, preferred_element_type=jnp.float32
    ).astype(jnp.bfloat16)
    rows_grad = jnp.dot(
        gather(rows, 1), sent, preferred_element_type=jnp.float32
    ).astype(jnp.bfloat16)
    rows_in_ref[...] = rows_in
    rows_grad_ref[...] = rows_grad
    proj_ref[...] = jnp.dot(
        rows_in, w_in_ref[...], preferred_element_type=jnp.float32
    ).astype(jnp.bfloat16)
    grad_ref[...] = contract_last(rows_grad, w_down_ref[...]).astype(jnp.bfloat16)


def total_of(refs):
    total = refs[0][...].astype(jnp.float32)
    for ref in refs[1:]:
        total = total + ref[...].astype(jnp.float32)
    return total


def backward_kernel(count, fold, *refs):
    w_in_ref, w_down_ref, hidden_ref, pair_ref, back_ref = refs[2 * count :]
    rows, half = back_ref.shape[0], hidden_ref.shape[1]
    projected = total_of(refs[:count])
    hidden_grad = total_of(refs[count : 2 * count])
    gate_part = projected[:, :half]
    up_part = projected[:, half:]
    sigmoid_gate = jax.nn.sigmoid(gate_part)
    swish = gate_part * sigmoid_gate
    hidden = (swish * up_part).astype(jnp.bfloat16)
    gate_grad = hidden_grad * up_part * sigmoid_gate * (1.0 + gate_part * (1.0 - sigmoid_gate))
    hidden_ref[...] = hidden
    pair_ref[:, :half] = gate_grad.astype(jnp.bfloat16)
    pair_ref[:, half:] = (hidden_grad * swish).astype(jnp.bfloat16)
    out_rows = jnp.dot(
        hidden, w_down_ref[...], preferred_element_type=jnp.float32
    ).astype(jnp.bfloat16)
    input_rows = contract_last(pair_ref[...], w_in_ref[...]).astype(jnp.bfloat16)
    back_ref[...] = (
        jnp.dot(spread(rows, 0, fold), out_rows, preferred_element_type=jnp.float32)
        + jnp.dot(spread(rows, 1, fold), input_rows, preferred_element_type=jnp.float32)
    ).astype(jnp.bfloat16)


def paired(table):
    groups = table.shape[0] // PACK
    order = [(g % 2) * (groups // 2) + g // 2 for g in range(groups)]
    return jnp.concatenate([table[g * PACK : (g + 1) * PACK] for g in order], axis=0)


def combine_kernel(pick_ref, gate_ref, *refs):
    out_ref, grad_ref = refs[-2:]
    back = together(refs[:-2])
    pick, gate = pick_ref[...], gate_ref[...]
    if len(refs) > 3:
        pick, gate = paired(pick), paired(gate)
    is_grad = part_of(back.shape[0]) == 1
    gate = jnp.where(is_grad, 0.0, gate)
    pick = jnp.where(is_grad, pick, 0.0).astype(jnp.bfloat16)
    high = gate.astype(jnp.bfloat16)
    rest = gate - high.astype(jnp.float32)
    middle = rest.astype(jnp.bfloat16)
    low = (rest - middle.astype(jnp.float32)).astype(jnp.bfloat16)
    total = contract_first(low, back) + contract_first(middle, back) + contract_first(high, back)
    out_ref[...] = total.astype(jnp.bfloat16)
    grad_ref[...] = contract_first(pick, back).astype(jnp.bfloat16)


def outer_kernel(left_ref, right_ref, out_ref):
    out_ref[...] = contract_first(left_ref[...], right_ref[...]).astype(jnp.bfloat16)


def outer(left, right, by_left, steps):
    depth, height = left.shape
    width = right.shape[1]
    move, stay = (lambda i: (0, i)), (lambda i: (0, 0))
    if by_left:
        block = (height // steps, width)
        specs = [pl.BlockSpec((depth, block[0]), move), pl.BlockSpec((depth, width), stay)]
        place = lambda i: (i, 0)
    else:
        block = (height, width // steps)
        specs = [pl.BlockSpec((depth, height), stay), pl.BlockSpec((depth, block[1]), move)]
        place = lambda i: (0, i)
    return pl.pallas_call(
        outer_kernel,
        grid=(steps,),
        in_specs=specs,
        out_specs=pl.BlockSpec(block, place),
        out_shape=jax.ShapeDtypeStruct((height, width), jnp.bfloat16),
        compiler_params=pltpu.CompilerParams(vmem_limit_bytes=VMEM_LIMIT),
        cost_estimate=pl.CostEstimate(
            flops=2 * depth * height * width, bytes_accessed=2 * height * width, transcendentals=0
        ),
    )(left, right)


def on_chip(array):
    return pltpu.with_memory_space_constraint(array, pltpu.VMEM)


def off_chip(array):
    return pltpu.with_memory_space_constraint(array, pltpu.HBM)


def contract_last(left, right):
    return lax.dot_general(
        left, right, (((1,), (1,)), ((), ())), preferred_element_type=jnp.float32
    )


def contract_first(left, right):
    return lax.dot_general(
        left, right, (((0,), (0,)), ((), ())), preferred_element_type=jnp.float32
    )


def flip(array, axis, members, step):
    return lax.ppermute(array, axis, [(i, i ^ step) for i in range(members)])


def exchange(packed, members, fold, meanwhile):
    rows, share = packed.shape
    if not fold:
        meanwhile(packed)
        return [
            lax.all_to_all(
                packed.reshape(members, PACK, share),
                "expert", split_axis=0, concat_axis=0, tiled=True,
            ).reshape(rows, share)
        ]
    got = flip(packed[rows // 2 :], "expert", members, 1)
    blocks = [packed, got]
    for s in range(1, members // 2):
        send = [packed[s * PACK : (s + 1) * PACK], got[s * PACK : (s + 1) * PACK]]
        blocks.append(flip(jnp.concatenate(send), "expert", members, 2 * s))
    meanwhile(got)
    return blocks


def pieces_over(pieces, axis, members):
    if members & (members - 1) or members > 4:
        return [lax.psum(pieces, axis)]
    found = [pieces]
    step = 1
    while step < members:
        if len(found) > 1:
            total = found[0].astype(jnp.float32) + found[1].astype(jnp.float32)
            found = [total.astype(jnp.bfloat16)]
        found.append(flip(found[0], axis, members, step))
        step *= 2
    return found


def body(members, tokens, upstream, expert_ids, gates, hot, w_in, w_down):
    expert_count = hot.shape[0]
    token_count, top_count = expert_ids.shape
    share = tokens.shape[1]
    half, wide = w_down.shape[1], w_in.shape[2]
    rows = expert_count * PACK
    row_count = expert_count * SLOTS
    fold = expert_count <= 8 and expert_count & (expert_count - 1) == 0
    own_in, own_down = w_in[0], w_down[0]
    params = pltpu.CompilerParams(vmem_limit_bytes=VMEM_LIMIT)
    anywhere = pl.BlockSpec(memory_space=pl.ANY)
    small = (expert_ids.T, gates.T, hot[None, :], tokens, upstream)
    packed, pick, gate = pl.pallas_call(
        functools.partial(dispatch_kernel, fold),
        in_specs=[anywhere] * 5,
        out_shape=[
            pltpu.VMEM((rows, share), jnp.bfloat16),
            pltpu.VMEM((rows, token_count), jnp.float32),
            pltpu.VMEM((rows, token_count), jnp.float32),
        ],
        scratch_shapes=[pltpu.VMEM(x.shape, x.dtype) for x in small]
        + [pltpu.SemaphoreType.DMA((5,))],
        compiler_params=params,
    )(*[off_chip(x) for x in small])
    near = []

    def load_weights(after):
        near.extend(
            pl.pallas_call(
                load_kernel,
                in_specs=[anywhere] * 3,
                out_shape=[
                    pltpu.VMEM(own_in.shape, jnp.bfloat16),
                    pltpu.VMEM(own_down.shape, jnp.bfloat16),
                ],
                scratch_shapes=[pltpu.SemaphoreType.DMA((2,))],
                compiler_params=params,
                cost_estimate=pl.CostEstimate(
                    flops=0, bytes_accessed=2 * (own_in.size + own_down.size), transcendentals=0
                ),
            )(on_chip(after), off_chip(own_in), off_chip(own_down))
        )

    sent = exchange(packed, expert_count, fold, load_weights)
    near_in, near_down = [on_chip(x) for x in near]
    proj, grad, rows_in, rows_grad = pl.pallas_call(
        forward_kernel,
        out_shape=[
            pltpu.VMEM((row_count, wide), jnp.bfloat16),
            pltpu.VMEM((row_count, half), jnp.bfloat16),
            pltpu.VMEM((row_count, share), jnp.bfloat16),
            pltpu.VMEM((row_count, share), jnp.bfloat16),
        ],
        compiler_params=params,
    )(*[on_chip(x) for x in sent], near_in, near_down)
    found = pieces_over(proj, "dp", members), pieces_over(grad, "dp", members)
    hidden, pair_grad, answer = pl.pallas_call(
        functools.partial(backward_kernel, len(found[0]), fold),
        out_shape=[
            pltpu.VMEM((row_count, half), jnp.bfloat16),
            pltpu.VMEM((row_count, wide), jnp.bfloat16),
            pltpu.VMEM((rows, share), jnp.bfloat16),
        ],
        compiler_params=params,
    )(*[on_chip(x) for x in found[0] + found[1]], near_in, near_down)
    grads = []

    def weight_grad(after):
        pair, _ = lax.optimization_barrier((pair_grad, after))
        grads.append(outer(rows_in, pair, False, 4))

    grad_down = outer(hidden, rows_grad, True, 4)
    back = exchange(answer, expert_count, fold, weight_grad)
    (grad_in,) = grads
    layer_out, token_grad = pl.pallas_call(
        combine_kernel,
        out_shape=[jax.ShapeDtypeStruct((token_count, share), jnp.bfloat16)] * 2,
        compiler_params=params,
    )(on_chip(pick), on_chip(gate), *[on_chip(x) for x in back])
    return (layer_out, token_grad, grad_in[None], grad_down[None])


def solution(mesh):
    return jax.shard_map(
        functools.partial(body, mesh.shape["dp"]),
        mesh=mesh,
        in_specs=(
            P("expert", "dp"),
            P("expert", "dp"),
            P("expert", None),
            P("expert", None),
            P(),
            P("expert", "dp", None),
            P("expert", None, "dp"),
        ),
        out_specs=(
            P("expert", "dp"),
            P("expert", "dp"),
            P("expert", "dp", None),
            P("expert", None, "dp"),
        ),
        check_vma=False,
    )
```

```python
import functools

import jax
import jax.numpy as jnp
from jax import lax
from jax.experimental import pallas as pl
from jax.experimental.pallas import tpu as pltpu
from jax.sharding import PartitionSpec as P

CAP = 2
SLOTS = 2 * CAP
PACK = 2 * SLOTS
LANES = 128
VMEM_LIMIT = 24 << 20


def select_table(ids, gates, hot, owner):
    top, tokens = ids.shape
    rows, experts = owner.shape[0], hot.shape[1]
    wanted = lax.broadcasted_iota(jnp.int32, (rows, 1), 0) % SLOTS
    chosen = jnp.zeros((rows, tokens), jnp.float32)
    gate = jnp.zeros((rows, tokens), jnp.float32)
    for k in range(top):
        hit = ids[k : k + 1, :] == owner
        chosen = jnp.where(hit, 1.0, chosen)
        gate = jnp.where(hit, gates[k : k + 1, :], gate)
    before = (
        lax.broadcasted_iota(jnp.int32, (tokens, tokens), 0)
        < lax.broadcasted_iota(jnp.int32, (tokens, tokens), 1)
    ).astype(jnp.float32).astype(jnp.bfloat16)
    occurrence = jnp.dot(
        chosen.astype(jnp.bfloat16), before, preferred_element_type=jnp.float32
    ).astype(jnp.int32)
    lane = lax.broadcasted_iota(jnp.int32, (rows, experts), 1)
    is_hot = jnp.max(jnp.where(lane == owner, hot, 0), axis=1, keepdims=True) == 1
    replica = jnp.where(is_hot, occurrence % 2, 0)
    rank = jnp.where(is_hot, occurrence // 2, occurrence)
    fills = (chosen > 0.0) & (rank < CAP) & (replica * CAP + rank == wanted)
    pick = jnp.where(fills, 1.0, 0.0)
    return pick, jnp.where(fills, gate, 0.0)


def part_of(rows):
    return (lax.broadcasted_iota(jnp.int32, (rows, 1), 0) % PACK) // SLOTS


def part_of(rows):
    return (lax.broadcasted_iota(jnp.int32, (rows, 1), 0) % PACK) // SLOTS


def owner_of(rows, fold, paired):
    group = lax.broadcasted_iota(jnp.int32, (rows, 1), 0) // PACK
    if not fold:
        return group
    if not paired:
        half = rows // PACK // 2
        group = 2 * (group % half) + group // half
    return lax.axis_index("expert") ^ group


def dispatch_kernel(
    fold, ids_hbm, gates_hbm, hot_hbm, tokens_hbm, upstream_hbm,
    packed_ref, pick_ref, gate_ref,
    ids_ref, gates_ref, hot_ref, tokens_ref, upstream_ref, sems,
):
    sources = (ids_hbm, gates_hbm, hot_hbm, tokens_hbm, upstream_hbm)
    targets = (ids_ref, gates_ref, hot_ref, tokens_ref, upstream_ref)
    copies = [
        pltpu.make_async_copy(source, target, sems.at[i])
        for i, (source, target) in enumerate(zip(sources, targets))
    ]
    for copy in copies:
        copy.start()
    for copy in copies[:3]:
        copy.wait()
    rows = packed_ref.shape[0]
    pick, gate = select_table(
        ids_ref[...], gates_ref[...], hot_ref[...], owner_of(rows, fold, False)
    )
    is_grad = part_of(rows) == 1
    pick_ref[...] = pick
    gate_ref[...] = gate
    pick = pick.astype(jnp.bfloat16)
    scale = jnp.sum(gate, axis=1, keepdims=True)
    for copy in copies[3:]:
        copy.wait()
    row_in = jnp.dot(pick, tokens_ref[...], preferred_element_type=jnp.float32)
    row_up = jnp.dot(pick, upstream_ref[...], preferred_element_type=jnp.float32)
    packed_ref[...] = jnp.where(is_grad, row_up * scale, row_in).astype(jnp.bfloat16)


def gather(rows, part):
    row = lax.broadcasted_iota(jnp.int32, (rows // 2, rows), 1)
    column = lax.broadcasted_iota(jnp.int32, (rows // 2, rows), 0)
    place = (column // SLOTS) * PACK + part * SLOTS + column % SLOTS
    return jnp.where(row == place, 1.0, 0.0).astype(jnp.bfloat16)


def spread(rows, part, fold):
    row = lax.broadcasted_iota(jnp.int32, (rows, rows // 2), 0)
    column = lax.broadcasted_iota(jnp.int32, (rows, rows // 2), 1)
    group = column // SLOTS
    if fold:
        group = (group % 2) * (rows // PACK // 2) + group // 2
    place = group * PACK + part * SLOTS + column % SLOTS
    return jnp.where(row == place, 1.0, 0.0).astype(jnp.bfloat16)


def load_kernel(after_ref, w_in_hbm, w_down_hbm, w_in_ref, w_down_ref, sems):
    loads = [
        pltpu.make_async_copy(w_in_hbm, w_in_ref, sems.at[0]),
        pltpu.make_async_copy(w_down_hbm, w_down_ref, sems.at[1]),
    ]
    for load in loads:
        load.start()
    for load in loads:
        load.wait()


def together(refs):
    if len(refs) == 1:
        return refs[0][...]
    parts = [refs[0][:PACK], refs[1][:PACK]] + [ref[...] for ref in refs[2:]]
    return jnp.concatenate(parts, axis=0)


def forward_kernel(*refs):
    w_in_ref, w_down_ref, proj_ref, grad_ref, rows_in_ref, rows_grad_ref = refs[-6:]
    sent = together(refs[:-6])
    rows = sent.shape[0]
    rows_in = jnp.dot(
        gather(rows, 0), sent, preferred_element_type=jnp.float32
    ).astype(jnp.bfloat16)
    rows_grad = jnp.dot(
        gather(rows, 1), sent, preferred_element_type=jnp.float32
    ).astype(jnp.bfloat16)
    rows_in_ref[...] = rows_in
    rows_grad_ref[...] = rows_grad
    proj_ref[...] = jnp.dot(
        rows_in, w_in_ref[...], preferred_element_type=jnp.float32
    ).astype(jnp.bfloat16)
    grad_ref[...] = contract_last(rows_grad, w_down_ref[...]).astype(jnp.bfloat16)


def total_of(refs):
    total = refs[0][...].astype(jnp.float32)
    for ref in refs[1:]:
        total = total + ref[...].astype(jnp.float32)
    return total


def activate_kernel(count, *refs):
    w_down_ref, hidden_ref, slope_ref, swish_ref, out_ref = refs[count:]
    projected = total_of(refs[:count])
    half = hidden_ref.shape[1]
    gate_part = projected[:, :half]
    up_part = projected[:, half:]
    sigmoid_gate = jax.nn.sigmoid(gate_part)
    swish = gate_part * sigmoid_gate
    hidden = (swish * up_part).astype(jnp.bfloat16)
    hidden_ref[...] = hidden
    swish_ref[...] = swish
    slope_ref[...] = up_part * sigmoid_gate * (1.0 + gate_part * (1.0 - sigmoid_gate))
    out_ref[...] = jnp.dot(
        hidden, w_down_ref[...], preferred_element_type=jnp.float32
    ).astype(jnp.bfloat16)


def backward_kernel(count, fold, *refs):
    slope_ref, swish_ref, out_ref, w_in_ref, pair_ref, back_ref = refs[count:]
    rows, half = back_ref.shape[0], slope_ref.shape[1]
    hidden_grad = total_of(refs[:count])
    pair_ref[:, :half] = (hidden_grad * slope_ref[...]).astype(jnp.bfloat16)
    pair_ref[:, half:] = (hidden_grad * swish_ref[...]).astype(jnp.bfloat16)
    input_rows = contract_last(pair_ref[...], w_in_ref[...]).astype(jnp.bfloat16)
    back_ref[...] = (
        jnp.dot(spread(rows, 0, fold), out_ref[...], preferred_element_type=jnp.float32)
        + jnp.dot(spread(rows, 1, fold), input_rows, preferred_element_type=jnp.float32)
    ).astype(jnp.bfloat16)


def paired(table):
    groups = table.shape[0] // PACK
    order = [(g % 2) * (groups // 2) + g // 2 for g in range(groups)]
    return jnp.concatenate([table[g * PACK : (g + 1) * PACK] for g in order], axis=0)


def combine_kernel(pick_ref, gate_ref, *refs):
    out_ref, grad_ref = refs[-2:]
    back = together(refs[:-2])
    pick, gate = pick_ref[...], gate_ref[...]
    if len(refs) > 3:
        pick, gate = paired(pick), paired(gate)
    is_grad = part_of(back.shape[0]) == 1
    gate = jnp.where(is_grad, 0.0, gate)
    pick = jnp.where(is_grad, pick, 0.0).astype(jnp.bfloat16)
    high = gate.astype(jnp.bfloat16)
    rest = gate - high.astype(jnp.float32)
    middle = rest.astype(jnp.bfloat16)
    low = (rest - middle.astype(jnp.float32)).astype(jnp.bfloat16)
    total = contract_first(low, back) + contract_first(middle, back) + contract_first(high, back)
    out_ref[...] = total.astype(jnp.bfloat16)
    grad_ref[...] = contract_first(pick, back).astype(jnp.bfloat16)


def blocks_of(height):
    size = LANES if height % LANES == 0 else height
    return [(start, size) for start in range(0, height, size)]


def outer_kernel(*refs):
    _, rows_in_ref, pair_ref, hidden_ref, rows_grad_ref, grad_in, grad_down = refs[:7]
    in_buffer, down_buffer, in_sems, down_sems = refs[7:]
    copies = []
    for left_ref, right_ref, buffer, target, sems in (
        (rows_in_ref, pair_ref, in_buffer, grad_in, in_sems),
        (hidden_ref, rows_grad_ref, down_buffer, grad_down, down_sems),
    ):
        right = right_ref[...]
        for i, (start, size) in enumerate(blocks_of(left_ref.shape[1])):
            place = pl.ds(start, size)
            buffer[place, :] = contract_first(
                left_ref[:, start : start + size], right
            ).astype(jnp.bfloat16)
            copies.append(
                pltpu.make_async_copy(buffer.at[place], target.at[place], sems.at[i])
            )
            copies[-1].start()
    for copy in copies:
        copy.wait()


def on_chip(array):
    return pltpu.with_memory_space_constraint(array, pltpu.VMEM)


def off_chip(array):
    return pltpu.with_memory_space_constraint(array, pltpu.HBM)


def contract_last(left, right):
    return lax.dot_general(
        left, right, (((1,), (1,)), ((), ())), preferred_element_type=jnp.float32
    )


def contract_first(left, right):
    return lax.dot_general(
        left, right, (((0,), (0,)), ((), ())), preferred_element_type=jnp.float32
    )


def flip(array, axis, members, step):
    return lax.ppermute(array, axis, [(i, i ^ step) for i in range(members)])


def exchange(packed, members, fold, meanwhile):
    rows, share = packed.shape
    if not fold:
        meanwhile(packed)
        return [
            lax.all_to_all(
                packed.reshape(members, PACK, share),
                "expert", split_axis=0, concat_axis=0, tiled=True,
            ).reshape(rows, share)
        ]
    got = flip(packed[rows // 2 :], "expert", members, 1)
    blocks = [packed, got]
    for s in range(1, members // 2):
        send = [packed[s * PACK : (s + 1) * PACK], got[s * PACK : (s + 1) * PACK]]
        blocks.append(flip(jnp.concatenate(send), "expert", members, 2 * s))
    meanwhile(got)
    return blocks


def pieces_over(pieces, axis, members):
    if members & (members - 1) or members > 4:
        return [lax.psum(pieces, axis)]
    found = [pieces]
    step = 1
    while step < members:
        if len(found) > 1:
            total = found[0].astype(jnp.float32) + found[1].astype(jnp.float32)
            found = [total.astype(jnp.bfloat16)]
        found.append(flip(found[0], axis, members, step))
        step *= 2
    return found


def body(members, tokens, upstream, expert_ids, gates, hot, w_in, w_down):
    expert_count = hot.shape[0]
    token_count, top_count = expert_ids.shape
    share = tokens.shape[1]
    half, wide = w_down.shape[1], w_in.shape[2]
    rows = expert_count * PACK
    row_count = expert_count * SLOTS
    fold = expert_count <= 8 and expert_count & (expert_count - 1) == 0
    own_in, own_down = w_in[0], w_down[0]
    params = pltpu.CompilerParams(vmem_limit_bytes=VMEM_LIMIT)
    anywhere = pl.BlockSpec(memory_space=pl.ANY)
    small = (expert_ids.T, gates.T, hot[None, :], tokens, upstream)
    packed, pick, gate = pl.pallas_call(
        functools.partial(dispatch_kernel, fold),
        in_specs=[anywhere] * 5,
        out_shape=[
            pltpu.VMEM((rows, share), jnp.bfloat16),
            pltpu.VMEM((rows, token_count), jnp.float32),
            pltpu.VMEM((rows, token_count), jnp.float32),
        ],
        scratch_shapes=[pltpu.VMEM(x.shape, x.dtype) for x in small]
        + [pltpu.SemaphoreType.DMA((5,))],
        compiler_params=params,
    )(*[off_chip(x) for x in small])
    near = []

    def load_weights(after):
        near.extend(
            pl.pallas_call(
                load_kernel,
                in_specs=[anywhere] * 3,
                out_shape=[
                    pltpu.VMEM(own_in.shape, jnp.bfloat16),
                    pltpu.VMEM(own_down.shape, jnp.bfloat16),
                ],
                scratch_shapes=[pltpu.SemaphoreType.DMA((2,))],
                compiler_params=params,
                cost_estimate=pl.CostEstimate(
                    flops=0, bytes_accessed=2 * (own_in.size + own_down.size), transcendentals=0
                ),
            )(on_chip(after), off_chip(own_in), off_chip(own_down))
        )

    sent = exchange(packed, expert_count, fold, load_weights)
    near_in, near_down = [on_chip(x) for x in near]
    proj, grad, rows_in, rows_grad = pl.pallas_call(
        forward_kernel,
        out_shape=[
            pltpu.VMEM((row_count, wide), jnp.bfloat16),
            pltpu.VMEM((row_count, half), jnp.bfloat16),
            pltpu.VMEM((row_count, share), jnp.bfloat16),
            pltpu.VMEM((row_count, share), jnp.bfloat16),
        ],
        compiler_params=params,
    )(*[on_chip(x) for x in sent], near_in, near_down)
    found = pieces_over(proj, "dp", members), pieces_over(grad, "dp", members)
    hidden, slope, swish, out_rows = pl.pallas_call(
        functools.partial(activate_kernel, len(found[0])),
        out_shape=[
            pltpu.VMEM((row_count, half), jnp.bfloat16),
            pltpu.VMEM((row_count, half), jnp.float32),
            pltpu.VMEM((row_count, half), jnp.float32),
            pltpu.VMEM((row_count, share), jnp.bfloat16),
        ],
        compiler_params=params,
    )(*[on_chip(x) for x in found[0]], near_down)
    pair_grad, answer = pl.pallas_call(
        functools.partial(backward_kernel, len(found[1]), fold),
        out_shape=[
            pltpu.VMEM((row_count, wide), jnp.bfloat16),
            pltpu.VMEM((rows, share), jnp.bfloat16),
        ],
        compiler_params=params,
    )(*[on_chip(x) for x in found[1] + [slope, swish, out_rows]], near_in)
    grads = []

    def weight_grads(after):
        operands = (after, rows_in, pair_grad, hidden, rows_grad)
        grads.extend(
            pl.pallas_call(
                outer_kernel,
                in_specs=[anywhere] + [pl.BlockSpec(memory_space=pltpu.VMEM)] * 4,
                out_specs=[anywhere] * 2,
                out_shape=[
                    pltpu.HBM(own_in.shape, jnp.bfloat16),
                    pltpu.HBM(own_down.shape, jnp.bfloat16),
                ],
                scratch_shapes=[
                    pltpu.VMEM(own_in.shape, jnp.bfloat16),
                    pltpu.VMEM(own_down.shape, jnp.bfloat16),
                    pltpu.SemaphoreType.DMA((len(blocks_of(share)),)),
                    pltpu.SemaphoreType.DMA((len(blocks_of(half)),)),
                ],
                compiler_params=params,
                cost_estimate=pl.CostEstimate(
                    flops=2 * row_count * (own_in.size + own_down.size),
                    bytes_accessed=2 * (own_in.size + own_down.size),
                    transcendentals=0,
                ),
            )(*[on_chip(x) for x in operands])
        )

    back = exchange(answer, expert_count, fold, weight_grads)
    grad_in, grad_down = grads
    layer_out, token_grad = pl.pallas_call(
        combine_kernel,
        out_shape=[jax.ShapeDtypeStruct((token_count, share), jnp.bfloat16)] * 2,
        compiler_params=params,
    )(on_chip(pick), on_chip(gate), *[on_chip(x) for x in back])
    return (layer_out, token_grad, grad_in[None], grad_down[None])


def solution(mesh):
    return jax.shard_map(
        functools.partial(body, mesh.shape["dp"]),
        mesh=mesh,
        in_specs=(
            P("expert", "dp"),
            P("expert", "dp"),
            P("expert", None),
            P("expert", None),
            P(),
            P("expert", "dp", None),
            P("expert", None, "dp"),
        ),
        out_specs=(
            P("expert", "dp"),
            P("expert", "dp"),
            P("expert", "dp", None),
            P("expert", None, "dp"),
        ),
        check_vma=False,
    )
```
